1024 devices in a mesh: seq: 64 (over y, z_lo), fsdp: 8 (over z_hi, x), grp: 2 (over core).
Axes of the slice: x: 4, y: 4, z: 32 (z_hi: 2, z_lo: 16; z = z_hi * 16 + z_lo), core: 2. Of those that a mesh axis runs over, the one named last changes fastest.
Arguments:
- queries: bfloat16 [1, 65536, 2048], P(None, ('seq', 'fsdp'), 'grp'), may hold values from -208 to 208
- encodings: bfloat16 [1, 1024, 2, 128, 896], P(None, ('seq', 'fsdp'), None, 'grp'), may hold values from -6 to 6
- neighbour_lengths: int32 [1, 1024, 2], P(None, ('seq', 'fsdp')), may hold values from 32 to 128
- key_weight: bfloat16 [896, 2048], P(None, 'grp'), may hold values from -0.1875 to 0.1875
- value_weight: bfloat16 [896, 2048], P(None, 'grp'), may hold values from -0.1875 to 0.1875
Outputs:
- attended: bfloat16 [1, 65536, 2048], P(None, ('seq', 'fsdp'), 'grp')
The draws below stay inside these ranges and needn't reach their ends.
All inputs are finite; a program needn't handle non-finite values.
Results may differ from the reference program's by a relative error of at most 0.011.
Values may be sent and summed in bfloat16 or wider, within the bound.
A program may use at most 32 MiB of HBM per device.

```python
import jax
import jax.numpy as jnp
from jax import lax

HEADS = 16
HEAD_DIM = 128
ENC_WIDTH = 896
GROUP = 64
NEIGH = 2
NB_LEN = 128
SEQS = 1
N_GROUPS = 1024
SEQ_LEN = 65536
ATT_WIDTH = 2048


def draw_queries(key, part):
    full_shape = (SEQS, SEQ_LEN, HEADS * HEAD_DIM)
    base_key = jax.random.fold_in(key, 0)
    values = jnp.clip(2.0 * jax.random.normal(base_key, full_shape, jnp.float32), -12.0, 12.0)
    return values.astype(jnp.bfloat16)


def set_ends(drawn, key, smallest, high):
    dims = drawn.shape
    index_at = [jax.random.randint(jax.random.fold_in(key, axis), (), 0, dims[axis]) for axis in range(len(dims))]
    drawn = drawn.at[tuple(index_at)].set(smallest)
    longest = dims.index(max(dims))
    index_at[longest] = (index_at[longest] + 1) % dims[longest]
    return drawn.at[tuple(index_at)].set(high)


def block_scale(rng, extent, shards, low, largest):
    loudness, own = 1.0, jax.random.fold_in(rng, 6)
    for dim, parts in shards:
        draws = jnp.exp(jax.random.uniform(jax.random.fold_in(own, dim), (parts,), jnp.float32, low / len(shards), largest / len(shards)))
        loudness = loudness * jnp.repeat(draws, extent[dim] // parts).reshape([-1 if axis == dim else 1 for axis in range(len(extent))])
    return loudness


def scatter_about(rng, shape, width, limit, cuts=(), held_as=jnp.bfloat16):
    array = width * jax.random.normal(rng, shape, jnp.float32)
    if cuts:
        array = array * block_scale(rng, shape, cuts, -0.22, 0.18)
    return jnp.clip(array, -limit, limit).astype(held_as)


def setup_inputs(seed: int = 0) -> dict:
    splits = jax.random.split(jax.random.key(seed), 6)
    return {
        "queries": draw_queries(jax.random.fold_in(splits[5], 71), 0),
        "encodings": scatter_about(splits[1], (SEQS, N_GROUPS, NEIGH, NB_LEN, ENC_WIDTH), 1.0, 6.0, ((1, 512), (3, 2))),
        "neighbour_lengths": set_ends(jax.random.randint(splits[2], (SEQS, N_GROUPS, NEIGH), NB_LEN // 4, NB_LEN + 1), jax.random.fold_in(splits[2], 1), NB_LEN // 4, NB_LEN).astype(jnp.int32),
        "key_weight": scatter_about(splits[3], (ENC_WIDTH, ATT_WIDTH), ENC_WIDTH ** -0.5, 0.1875, ((1, 2),)),
        "value_weight": scatter_about(splits[4], (ENC_WIDTH, ATT_WIDTH), ENC_WIDTH ** -0.5, 0.1875, ((1, 2),)),
    }


mask_fill = -1.0e30


def reference(queries, encodings, neighbour_lengths, key_weight, value_weight):
    total_cols = HEADS * HEAD_DIM
    softmax_scale = HEAD_DIM ** -0.5
    lead_zeros = jnp.zeros((SEQS, 1, total_cols), jnp.bfloat16)
    trail_zeros = jnp.zeros((SEQS, GROUP - 1, total_cols), jnp.bfloat16)
    padded = jnp.concatenate([lead_zeros, queries, trail_zeros], axis=1)
    padded = jnp.moveaxis(padded.reshape(SEQS, N_GROUPS + 1, GROUP, total_cols), 1, 0)

    def one_block(block_index):
        block_queries = lax.dynamic_index_in_dim(padded, block_index, 0, keepdims=False)
        source = jnp.maximum(block_index - 1, 0).astype(jnp.int32)
        enc_rows = lax.dynamic_index_in_dim(encodings, source, 1, keepdims=False)
        lengths = lax.dynamic_index_in_dim(neighbour_lengths, source, 1, keepdims=False)
        flat_rows = enc_rows.reshape(SEQS * NEIGH * NB_LEN, ENC_WIDTH)
        key_rows = jnp.dot(flat_rows, key_weight, preferred_element_type=jnp.float32).astype(jnp.bfloat16)
        value_rows = jnp.dot(flat_rows, value_weight, preferred_element_type=jnp.float32).astype(jnp.bfloat16)
        key_rows = key_rows.reshape(SEQS, NEIGH * NB_LEN, HEADS, HEAD_DIM)
        value_rows = value_rows.reshape(SEQS, NEIGH * NB_LEN, HEADS, HEAD_DIM)
        query_heads = block_queries.reshape(SEQS, GROUP, HEADS, HEAD_DIM)
        scores = jnp.einsum("bqhd,bkhd->bhqk", query_heads.astype(jnp.float32), key_rows.astype(jnp.float32)) * softmax_scale
        position = lax.broadcasted_iota(jnp.int32, (SEQS, NEIGH, NB_LEN), 2)
        key_live = (position < lengths[:, :, None]).reshape(SEQS, 1, 1, NEIGH * NB_LEN)
        scores = jnp.where(key_live, scores, mask_fill)
        row_max = jnp.max(scores, axis=-1, keepdims=True)
        weights = jnp.exp(scores - row_max)
        attention = (weights / jnp.sum(weights, axis=-1, keepdims=True)).astype(jnp.bfloat16)
        attended = jnp.einsum("bhqk,bkhd->bqhd", attention.astype(jnp.float32), value_rows.astype(jnp.float32))
        attended = attended.astype(jnp.bfloat16).reshape(SEQS, GROUP, total_cols)
        return jnp.where(block_index > 0, attended, jnp.zeros_like(attended))

    blocks = lax.map(one_block, jnp.arange(N_GROUPS + 1, dtype=jnp.int32))
    joined = jnp.moveaxis(blocks, 0, 1).reshape(SEQS, (N_GROUPS + 1) * GROUP, total_cols)
    return joined[:, 1:1 + SEQ_LEN]
```

```python
import jax
import jax.numpy as jnp
from jax import lax
from jax.sharding import PartitionSpec as P

HEAD_DIM = 128


mask_fill = -1e30


def shifted(array, axis, by):
    size = lax.axis_size(axis)
    pairs = [(i, i + by) for i in range(size) if 0 <= i + by < size]
    return lax.ppermute(array, axis, pairs)


def attend_blocks(query_blocks, key_value, lengths):
    seq_count, block_count, row_count, col_count = query_blocks.shape
    head_count = col_count // HEAD_DIM
    key_count = key_value.shape[3] * key_value.shape[4]
    softmax_scale = HEAD_DIM ** (-0.5)
    query_heads = query_blocks.reshape(seq_count, block_count, row_count, head_count, HEAD_DIM)
    key_rows = key_value[0].reshape(seq_count, block_count, key_count, head_count, HEAD_DIM)
    value_rows = key_value[1].reshape(seq_count, block_count, key_count, head_count, HEAD_DIM)
    scores = (
        jnp.einsum("bnqhd,bnkhd->bnhqk", query_heads, key_rows, preferred_element_type=jnp.float32)
        * softmax_scale
    )
    position = lax.broadcasted_iota(jnp.float32, key_value.shape[1:5], 3)
    key_live = (position < lengths[..., None]).reshape(seq_count, block_count, 1, 1, key_count)
    scores = jnp.where(key_live, scores, mask_fill)
    row_max = jnp.max(scores, axis=-1, keepdims=True)
    weights = jnp.exp(scores - row_max)
    attention = (weights / jnp.sum(weights, axis=-1, keepdims=True)).astype(jnp.bfloat16)
    attended = jnp.einsum(
        "bnhqk,bnkhd->bnqhd", attention, value_rows, preferred_element_type=jnp.float32
    )
    return attended.astype(jnp.bfloat16).reshape(seq_count, block_count * row_count, col_count)


def attend_padded(queries, all_pairs, all_lengths, group_count, group_len):
    seq_count, tok_count, col_count = queries.shape
    lead_zeros = jnp.zeros((seq_count, 1, col_count), jnp.bfloat16)
    trail_zeros = jnp.zeros((seq_count, group_len - 1, col_count), jnp.bfloat16)
    padded = jnp.concatenate([lead_zeros, queries, trail_zeros], axis=1)
    blocks = padded.reshape(seq_count, group_count + 1, group_len, col_count)
    attended = attend_blocks(blocks, all_pairs, all_lengths)
    return attended[:, 1 : 1 + tok_count]


def shards(queries, encodings, neighbour_lengths, key_weight, value_weight):
    seq_count, tok_count, col_count = queries.shape
    group_count = encodings.shape[1]
    group_len = tok_count // group_count
    enc_width = encodings.shape[4]
    last_rows = encodings[:, group_count - 1 :]
    last_lengths = neighbour_lengths[:, group_count - 1 :]
    prev_rows, prev_lengths = shifted((last_rows, last_lengths), ("seq", "fsdp"), 1)

    def project(rows):
        rows = lax.all_gather(rows, "grp", axis=3, tiled=True)
        flat_rows = rows.reshape(-1, enc_width)
        pair = [
            jnp.dot(flat_rows, weight, preferred_element_type=jnp.float32).astype(jnp.bfloat16)
            for weight in (key_weight, value_weight)
        ]
        return jnp.stack(pair).reshape((2,) + rows.shape[:4] + (col_count,))

    all_pairs = jnp.concatenate([project(prev_rows), project(encodings)], axis=2)
    all_lengths = jnp.concatenate([prev_lengths, neighbour_lengths], axis=1).astype(jnp.float32)
    return attend_padded(queries, all_pairs, all_lengths, group_count, group_len)


def solution(mesh):
    placed = (
        P(None, ("seq", "fsdp"), "grp"),
        P(None, ("seq", "fsdp"), None, "grp", None),
        P(None, ("seq", "fsdp"), None),
        P(None, "grp"),
        P(None, "grp"),
    )
    return jax.shard_map(
        shards,
        mesh=mesh,
        in_specs=placed,
        out_specs=P(None, ("seq", "fsdp"), "grp"),
        check_vma=False,
    )
```

```python
import jax
import jax.numpy as jnp
from jax import lax
from jax.experimental import pallas as pl
from jax.experimental.pallas import tpu as pltpu
from jax.sharding import PartitionSpec as P

HEAD_DIM = 128
GROUP_LEN = 64
MASK_FILL = -1e30
MESH_ID = pl.DeviceIdType.MESH

X, Z, HALF = 4, 32, 16
COLUMN_PIECES = {3: 2, 0: 2, 2: 2, 1: 2}
LEGS = (4, 4, 4, 4)
PIECE_ROWS = 8


def piece_table():
    table, at = {}, 0
    most = max(COLUMN_PIECES.values())
    for j in range(most):
        for column, count in COLUMN_PIECES.items():
            if j < count:
                for way in (0, 1):
                    table[column, way, j] = at
                    at += 1
    return table


PIECES = piece_table()
N_PIECES = len(PIECES)
MOST = max(COLUMN_PIECES.values())
N_LEGS = len(LEGS)
SIGN = (1, -1)


def kernel(
    q_hbm, enc_hbm, len_hbm, kw_hbm, vw_hbm, out_ref,
    q_ref, kw_ref, vw_ref, len_ref, prev_len, rows_ref, prev_ref, keys_ref, vals_ref, own_out,
    relay, len_relay,
    in_sem, out_sem, relay_sem, forward_sem, prev_sem, swap_send, swap_recv,
    len_send, len_recv, own_send, own_recv,
):
    seq, fsdp, core = lax.axis_index("seq"), lax.axis_index("fsdp"), lax.axis_index("grp")
    x, y = lax.rem(fsdp, X), lax.div(seq, HALF)
    z = lax.rem(seq, HALF) + HALF * lax.div(fsdp, X)
    other = 1 - core

    def device(to_x, to_y, to_z, to_core):
        return (to_y * HALF + lax.rem(to_z, HALF), lax.div(to_z, HALF) * X + to_x, to_core)

    def wrap(at):
        return lax.rem(at + 2 * Z, Z)

    def target_of(origin):
        return jnp.where(origin < HALF, origin + HALF, origin - (HALF - 1))

    def origin_of(target):
        return jnp.where(target < HALF, target + (HALF - 1), target - HALF)

    sibling = device(x, y, z, other)
    reached = [sum(LEGS[:leg]) for leg in range(N_LEGS + 1)]
    last_z = (z == Z - 1)
    crosses_y = last_z & (y < X - 1)
    has_prev = (x > 0) | (z > 0) | (y > 0)
    columns = list(COLUMN_PIECES)
    far = reached[N_LEGS - 1]

    def remote(src, dst, send, recv, to):
        return pltpu.make_async_remote_copy(
            src_ref=src, dst_ref=dst, send_sem=send, recv_sem=recv, device_id=to, device_id_type=MESH_ID
        )

    def arrived(dst, recv):
        remote(dst, dst, own_send, recv, sibling).wait_recv()

    def left(src, send):
        remote(src, src, send, own_recv, sibling).wait_send()

    barrier = pltpu.get_barrier_semaphore()

    def greet(who):
        pl.semaphore_signal(barrier, 1, device_id=who, device_id_type=MESH_ID)

    greet(sibling)

    @pl.when(x > 0)
    def _():
        greet(device(x - 1, y, z, core))

    for column in columns:
        if column != X - 1:

            @pl.when(x == column)
            def _():
                greet(device(X - 1, y, z, core))

    on_column = (x == columns[0])
    for column in columns[1:]:
        on_column = on_column | (x == column)

    @pl.when(on_column)
    def _():
        for way in (0, 1):
            greet(device(x, y, wrap(z - SIGN[way] * LEGS[0]), core))

    @pl.when((x == 0) & (z > 0))
    def _():
        for column in columns:
            for way in (0, 1):
                greet(device(column, y, wrap(origin_of(z) + SIGN[way] * far), core))

    @pl.when((x == 0) & (z == 0) & (y > 0))
    def _():
        for column in columns:
            greet(device(column, y - 1, Z - 1, core))

    rows_in = pltpu.make_async_copy(enc_hbm.at[0], rows_ref.at[core], in_sem.at[0])
    kw_in = pltpu.make_async_copy(kw_hbm, kw_ref, in_sem.at[1])
    vw_in = pltpu.make_async_copy(vw_hbm, vw_ref, in_sem.at[2])
    q_in = pltpu.make_async_copy(q_hbm.at[0], q_ref, in_sem.at[3])
    len_in = pltpu.make_async_copy(len_hbm.at[0], len_ref, in_sem.at[4])
    for copy in (rows_in, len_in, kw_in, vw_in, q_in):
        copy.start()

    def one(condition, count=1):
        return jnp.where(condition, count, 0)

    peers = 1 + one(x < X - 1) + one(x == X - 1, len(columns) - 1)
    column_peers = 2 + one(crosses_y)
    for way in (0, 1):
        column_peers = column_peers + one(wrap(z - SIGN[way] * far) != Z - 1)
    pl.semaphore_wait(barrier, peers + jnp.where(on_column, column_peers, 0))

    def last_rows(piece):
        at = piece * PIECE_ROWS
        return rows_ref.at[core, 1, at // GROUP_LEN, pl.ds(at % GROUP_LEN, PIECE_ROWS)]

    def prev_rows(half, piece):
        return prev_ref.at[half, pl.ds(piece * PIECE_ROWS, PIECE_ROWS)]

    def to_prev(piece, src, send, to):
        return remote(src, prev_rows(core, piece), send, prev_sem.at[piece], to)

    def relay_at(stage, way, j):
        return relay.at[stage, way, pl.ds(j * PIECE_ROWS, PIECE_ROWS)]

    def lens_to_prev(src, send, to):
        return remote(src, prev_len, send, len_recv.at[N_LEGS], to)

    rows_in.wait()
    len_in.wait()
    own_swap = remote(rows_ref.at[core], rows_ref.at[core], own_send, own_recv, sibling)

    @pl.when(x == X - 1)
    def _():
        for (column, way, j), piece in PIECES.items():
            src, send = last_rows(piece), out_sem.at[piece]
            if column != X - 1:

                @pl.when((z < Z - 1) | (y < X - 1))
                def _():
                    remote(
                        src, relay_at(0, way, j), send, relay_sem.at[0, way, j], device(column, y, z, core)
                    ).start()

            else:

                @pl.when(z < Z - 1)
                def _():
                    remote(
                        src, relay_at(1, way, j), send, relay_sem.at[1, way, j],
                        device(column, y, wrap(z + SIGN[way] * LEGS[0]), core),
                    ).start()

                @pl.when(crosses_y)
                def _():
                    to_prev(piece, src, send, device(0, y + 1, 0, core)).start()

        @pl.when(z < Z - 1)
        def _():
            remote(
                len_ref, len_relay.at[1], len_send.at[0], len_recv.at[1],
                device(X - 1, y, wrap(z + LEGS[0]), core),
            ).start()

        @pl.when(crosses_y)
        def _():
            lens_to_prev(len_ref, len_send.at[0], device(0, y + 1, 0, core)).start()

    @pl.when(x < X - 1)
    def _():
        to = device(x + 1, y, z, core)
        for piece in range(N_PIECES):
            to_prev(piece, last_rows(piece), out_sem.at[piece], to).start()
        lens_to_prev(len_ref, len_send.at[0], to).start()

    own_swap.start()

    row_in_keys = lax.broadcasted_iota(jnp.int32, (1, 4 * GROUP_LEN), 1)
    key_position = (row_in_keys // (2 * GROUP_LEN)) * GROUP_LEN + row_in_keys % GROUP_LEN
    key_neighbour = (row_in_keys // GROUP_LEN) % 2

    def key_live(lens):
        length = jnp.where(
            key_neighbour == 0,
            jnp.broadcast_to(lens[:, 0:1], row_in_keys.shape),
            jnp.broadcast_to(lens[:, 1:2], row_in_keys.shape),
        )
        return key_position < length

    def project(rows, slot):
        def columns_of(tile, carry):
            at = pl.ds(pl.multiple_of(tile * 256, 256), 256)
            keys_ref[slot, :, at] = jnp.dot(
                rows, kw_ref[:, at], preferred_element_type=jnp.float32
            ).astype(jnp.bfloat16)
            vals_ref[slot, :, at] = jnp.dot(
                rows, vw_ref[:, at], preferred_element_type=jnp.float32
            ).astype(jnp.bfloat16)
            return carry

        lax.fori_loop(0, kw_ref.shape[1] // 256, columns_of, 0)

    def attend(head, first, count, slot, live):
        at = pl.ds(head * HEAD_DIM, HEAD_DIM)
        scores = lax.dot_general(
            q_ref[first : first + count, at], keys_ref[slot, :, at],
            (((1,), (1,)), ((), ())), preferred_element_type=jnp.float32,
        ) * HEAD_DIM ** (-0.5)
        scores = jnp.where(live, scores, MASK_FILL)
        weights = jnp.exp(scores - jnp.max(scores, axis=-1, keepdims=True))
        attention = (weights / jnp.sum(weights, axis=-1, keepdims=True)).astype(jnp.bfloat16)
        return jnp.dot(attention, vals_ref[slot, :, at], preferred_element_type=jnp.float32).astype(
            jnp.bfloat16
        )

    n_heads = q_ref.shape[1] // HEAD_DIM

    def own_rows(group):
        return rows_ref[:, group].reshape(4 * GROUP_LEN, rows_ref.shape[-1])

    def step_own_project(group):
        if group == 0:
            kw_in.wait()
            vw_in.wait()
            arrived(rows_ref.at[other], own_recv)
        project(own_rows(group), group)

    def step_own_attend():
        q_in.wait()
        lens = len_ref[...]
        live0, live1 = key_live(lens[0:1]), key_live(lens[1:2])
        row = lax.broadcasted_iota(jnp.int32, (2 * GROUP_LEN, HEAD_DIM), 0)
        for head in range(n_heads):
            at = pl.ds(head * HEAD_DIM, HEAD_DIM)
            mid = attend(head, 0, 2 * GROUP_LEN, 0, live0)
            end = attend(head, GROUP_LEN, GROUP_LEN, 1, live1)
            end = jnp.concatenate([mid[:GROUP_LEN], end], axis=0)
            merged = jnp.where(row < 2 * GROUP_LEN - 1, mid, end)
            own_out[:, at] = merged

    def own_work(step):
        if step == 0:
            step_own_project(0)
        elif step == 1:
            step_own_project(1)
        elif step == 2:
            step_own_attend()

    def forward(stage, column):
        for j in range(COLUMN_PIECES[column]):
            for way in (0, 1):
                piece = PIECES[column, way, j]
                origin = wrap(z - SIGN[way] * reached[stage])
                src, send = relay_at(stage, way, j), forward_sem.at[stage, way, j]
                onward = origin != Z - 1

                @pl.when(onward)
                def _():
                    arrived(src, relay_sem.at[stage, way, j])
                    if stage < N_LEGS - 1:
                        remote(
                            src, relay_at(stage + 1, way, j), send, relay_sem.at[stage + 1, way, j],
                            device(column, y, wrap(z + SIGN[way] * LEGS[stage]), core),
                        ).start()
                    else:
                        to_prev(piece, src, send, device(0, y, target_of(origin), core)).start()

                if stage == 0:

                    @pl.when(crosses_y)
                    def _():
                        arrived(src, relay_sem.at[stage, way, j])
                        to_prev(piece, src, send, device(0, y + 1, 0, core)).start()

        if column == X - 1:
            origin = wrap(z - reached[stage])

            @pl.when(origin != Z - 1)
            def _():
                arrived(len_relay.at[stage], len_recv.at[stage])
                if stage < N_LEGS - 1:
                    remote(
                        len_relay.at[stage], len_relay.at[stage + 1], len_send.at[stage],
                        len_recv.at[stage + 1], device(column, y, wrap(z + LEGS[stage]), core),
                    ).start()
                else:
                    lens_to_prev(
                        len_relay.at[stage], len_send.at[stage], device(0, y, target_of(origin), core)
                    ).start()

    def settle(stage, column):
        for j in range(COLUMN_PIECES[column]):
            for way in (0, 1):
                origin = wrap(z - SIGN[way] * reached[stage])
                sent = origin != Z - 1
                if stage == 0:
                    sent = sent | crosses_y

                @pl.when(sent)
                def _():
                    left(relay_at(stage, way, j), forward_sem.at[stage, way, j])

        if column == X - 1:

            @pl.when(wrap(z - reached[stage]) != Z - 1)
            def _():
                left(len_relay.at[stage], len_send.at[stage])

    for stage in range(N_LEGS):
        for column in columns:
            if stage > 0 or column != X - 1:

                @pl.when(x == column)
                def _():
                    forward(stage, column)

        own_work(stage)

    @pl.when(has_prev)
    def _():
        for piece in range(N_PIECES):
            arrived(prev_rows(core, piece), prev_sem.at[piece])
            remote(
                prev_rows(core, piece), prev_rows(core, piece), swap_send.at[piece], swap_recv.at[piece], sibling
            ).start()
        arrived(prev_len, len_recv.at[N_LEGS])
        for piece in range(N_PIECES):
            arrived(prev_rows(other, piece), swap_recv.at[piece])

        project(prev_ref[...].reshape(4 * GROUP_LEN, prev_ref.shape[-1]), 2)
        live = key_live(prev_len[1:2])
        row = lax.broadcasted_iota(jnp.int32, (GROUP_LEN, HEAD_DIM), 0)
        for head in range(n_heads):
            at = pl.ds(head * HEAD_DIM, HEAD_DIM)
            first = attend(head, 0, GROUP_LEN, 2, live)
            out_ref[0, :GROUP_LEN, at] = jnp.where(row < GROUP_LEN - 1, first, own_out[:GROUP_LEN, at])

    @pl.when(jnp.logical_not(has_prev))
    def _():
        row = lax.broadcasted_iota(jnp.int32, (GROUP_LEN, own_out.shape[1]), 0)
        out_ref[0, :GROUP_LEN] = jnp.where(row < GROUP_LEN - 1, jnp.zeros_like(row, jnp.bfloat16), own_out[:GROUP_LEN])

    out_ref[0, GROUP_LEN:] = own_out[GROUP_LEN:]

    left(rows_ref.at[core], own_send)

    @pl.when((x < X - 1) | (z < Z - 1) | (y < X - 1))
    def _():
        for piece in range(N_PIECES):
            left(last_rows(piece), out_sem.at[piece])
        left(len_ref, len_send.at[0])

    for stage in range(N_LEGS):
        for column in columns:
            if stage > 0 or column != X - 1:

                @pl.when(x == column)
                def _():
                    settle(stage, column)

    @pl.when(has_prev)
    def _():
        for piece in range(N_PIECES):
            left(prev_rows(core, piece), swap_send.at[piece])


def shards(queries, encodings, neighbour_lengths, key_weight, value_weight):
    _, group_count, neighbours, half_rows, enc_width = encodings.shape
    tok_count, col_count = queries.shape[1:]
    bf16 = jnp.bfloat16
    anywhere = pl.BlockSpec(memory_space=pl.ANY)
    dma = pltpu.SemaphoreType.DMA
    return pl.pallas_call(
        kernel,
        out_shape=jax.ShapeDtypeStruct(queries.shape, bf16),
        in_specs=[anywhere] * 5,
        out_specs=pl.BlockSpec(memory_space=pltpu.VMEM),
        scratch_shapes=[
            pltpu.VMEM((tok_count, col_count), bf16),
            pltpu.VMEM(key_weight.shape, bf16),
            pltpu.VMEM(value_weight.shape, bf16),
            pltpu.VMEM((group_count, neighbours), jnp.int32),
            pltpu.VMEM((group_count, neighbours), jnp.int32),
            pltpu.VMEM((2, group_count, neighbours, half_rows, enc_width), bf16),
            pltpu.VMEM((2, neighbours * half_rows, enc_width), bf16),
            pltpu.VMEM((3, 2 * neighbours * half_rows, col_count), bf16),
            pltpu.VMEM((3, 2 * neighbours * half_rows, col_count), bf16),
            pltpu.VMEM((tok_count, col_count), bf16),
            pltpu.VMEM((N_LEGS, 2, MOST * PIECE_ROWS, enc_width), bf16),
            pltpu.VMEM((N_LEGS, group_count, neighbours), jnp.int32),
            dma((5,)),
            dma((N_PIECES,)),
            dma((N_LEGS, 2, MOST)),
            dma((N_LEGS, 2, MOST)),
            dma((N_PIECES,)),
            dma((N_PIECES,)),
            dma((N_PIECES,)),
            dma((N_LEGS,)),
            dma((N_LEGS + 1,)),
            dma,
            dma,
        ],
        compiler_params=pltpu.CompilerParams(
            collective_id=0, has_side_effects=True, vmem_limit_bytes=56 * 2**20
        ),
        name="attend_neighbours",
    )(queries, encodings, neighbour_lengths, key_weight, value_weight)


def solution(mesh):
    placed = (
        P(None, ("seq", "fsdp"), "grp"),
        P(None, ("seq", "fsdp"), None, "grp", None),
        P(None, ("seq", "fsdp"), None),
        P(None, "grp"),
        P(None, "grp"),
    )
    return jax.shard_map(
        shards,
        mesh=mesh,
        in_specs=placed,
        out_specs=P(None, ("seq", "fsdp"), "grp"),
        check_vma=False,
    )
```

```python
import jax
import jax.numpy as jnp
from jax import lax
from jax.experimental import pallas as pl
from jax.experimental.pallas import tpu as pltpu
from jax.sharding import PartitionSpec as P

HEAD_DIM = 128
GROUP_LEN = 64
MASK_FILL = -1e30
MESH_ID = pl.DeviceIdType.MESH

X, Z, HALF = 4, 32, 16
COLUMN_PIECES = {3: 4, 0: 4, 2: 4, 1: 4}
HOPS = (((0, 8, 8), (18, 22, 2)), ((0, 4, -4), (4, 8, 8), (18, 22, 2)))
PIECE_ROWS = 8
PIECES = {}
for _j in range(max(COLUMN_PIECES.values())):
    for _column, _count in COLUMN_PIECES.items():
        if _j < _count:
            PIECES[_column, _j] = len(PIECES)
N_PIECES = len(PIECES)
MOST = max(COLUMN_PIECES.values())


def kernel(
    q_hbm, enc_hbm, len_hbm, kw_hbm, vw_hbm, out_ref,
    q_ref, kw_ref, vw_ref, len_ref, prev_len, rows_ref, prev_ref, keys_ref, vals_ref, own_out,
    relay, len_relay,
    in_sem, out_sem, relay_sem, forward_sem, prev_sem, swap_send, swap_recv,
    len_send, len_recv, own_send, own_recv,
):
    seq, fsdp, core = lax.axis_index("seq"), lax.axis_index("fsdp"), lax.axis_index("grp")
    x, y = lax.rem(fsdp, X), lax.div(seq, HALF)
    z = lax.rem(seq, HALF) + HALF * lax.div(fsdp, X)
    other = 1 - core

    def device(to_x, to_y, to_z, to_core):
        return (to_y * HALF + lax.rem(to_z, HALF), lax.div(to_z, HALF) * X + to_x, to_core)

    sibling = device(x, y, z, other)
    last_z = (z == Z - 1)
    crosses_y = last_z & (y < X - 1)
    has_prev = (x > 0) | (z > 0) | (y > 0)
    columns = list(COLUMN_PIECES)

    def wrap(at):
        return lax.rem(at + Z, Z)

    def hop_of(origin, way):
        hop = jnp.zeros_like(origin)
        for first, end, by in HOPS[way]:
            hop = jnp.where((origin >= first) & (origin < end), by, hop)
        return hop

    def passed_by(way):
        origin = jnp.full_like(z, Z)
        for first, end, by in HOPS[way]:
            at = wrap(z - by)
            origin = jnp.where((at >= first) & (at < end), at, origin)
        return origin

    hops = [hop_of(z, way) for way in (0, 1)]
    direct = [(hop == 0) & (z < Z - 1) for hop in hops]
    loops = [hop != 0 for hop in hops]
    onward = [wrap(z + hop) for hop in hops]
    passed = [passed_by(way) for way in (0, 1)]
    passes = [origin < Z for origin in passed]

    def target_of(origin):
        return jnp.where(origin < HALF, origin + HALF, origin - (HALF - 1))

    def origin_of(target):
        return jnp.where(target < HALF, target + (HALF - 1), target - HALF)

    def remote(src, dst, send, recv, to):
        return pltpu.make_async_remote_copy(
            src_ref=src, dst_ref=dst, send_sem=send, recv_sem=recv, device_id=to, device_id_type=MESH_ID
        )

    def arrived(dst, recv):
        remote(dst, dst, own_send, recv, sibling).wait_recv()

    def left(src, send):
        remote(src, src, send, own_recv, sibling).wait_send()

    barrier = pltpu.get_barrier_semaphore()

    def greet(who):
        pl.semaphore_signal(barrier, 1, device_id=who, device_id_type=MESH_ID)

    greet(sibling)

    @pl.when(x > 0)
    def _():
        greet(device(x - 1, y, z, core))

    for column in columns:
        if column != X - 1:

            @pl.when(x == column)
            def _():
                greet(device(X - 1, y, z, core))

    on_column = (x == columns[0])
    for column in columns[1:]:
        on_column = on_column | (x == column)

    for way in (0, 1):

        @pl.when(on_column & passes[way])
        def _():
            greet(device(x, y, passed[way], core))

    @pl.when((x == 0) & (z > 0))
    def _():
        origin = origin_of(z)
        for column in columns:
            for way in (0, 1):
                greet(device(column, y, wrap(origin + hop_of(origin, way)), core))

    @pl.when((x == 0) & (z == 0) & (y > 0))
    def _():
        for column in columns:
            greet(device(column, y - 1, Z - 1, core))

    rows_in = pltpu.make_async_copy(enc_hbm.at[0], rows_ref.at[core], in_sem.at[0])
    kw_in = pltpu.make_async_copy(kw_hbm, kw_ref, in_sem.at[1])
    vw_in = pltpu.make_async_copy(vw_hbm, vw_ref, in_sem.at[2])
    q_in = pltpu.make_async_copy(q_hbm.at[0], q_ref, in_sem.at[3])
    len_in = pltpu.make_async_copy(len_hbm.at[0], len_ref, in_sem.at[4])
    for copy in (rows_in, len_in, kw_in, vw_in, q_in):
        copy.start()

    def one(condition, count=1):
        return jnp.where(condition, count, 0)

    peers = 1 + one(x < X - 1) + one(x == X - 1, len(columns) - 1)
    column_peers = one(crosses_y)
    for way in (0, 1):
        column_peers = column_peers + one(z < Z - 1) + one(passes[way])
    pl.semaphore_wait(barrier, peers + jnp.where(on_column, column_peers, 0))

    def last_rows(piece):
        at = piece * PIECE_ROWS
        return rows_ref.at[core, 1, at // GROUP_LEN, pl.ds(at % GROUP_LEN, PIECE_ROWS)]

    def prev_rows(half, piece):
        return prev_ref.at[half, pl.ds(piece * PIECE_ROWS, PIECE_ROWS)]

    def to_prev(piece, src, send, to):
        return remote(src, prev_rows(core, piece), send, prev_sem.at[piece], to)

    def relay_at(stage, j):
        return relay.at[stage, pl.ds(j * PIECE_ROWS, PIECE_ROWS)]

    def lens_to_prev(src, send, to):
        return remote(src, prev_len, send, len_recv.at[0], to)

    rows_in.wait()
    len_in.wait()
    own_swap = remote(rows_ref.at[core], rows_ref.at[core], own_send, own_recv, sibling)

    @pl.when(x == X - 1)
    def _():
        for (column, j), piece in PIECES.items():
            src, send, way = last_rows(piece), out_sem.at[piece], j % 2
            if column != X - 1:

                @pl.when((z < Z - 1) | (y < X - 1))
                def _():
                    to = device(column, y, z, core)
                    remote(src, relay_at(0, j), send, relay_sem.at[0, j], to).start()

            else:

                @pl.when(direct[way])
                def _():
                    to_prev(piece, src, send, device(0, y, target_of(z), core)).start()

                @pl.when(loops[way])
                def _():
                    to = device(column, y, onward[way], core)
                    remote(src, relay_at(1, j), send, relay_sem.at[1, j], to).start()

                @pl.when(crosses_y)
                def _():
                    to_prev(piece, src, send, device(0, y + 1, 0, core)).start()

        @pl.when(direct[0])
        def _():
            lens_to_prev(len_ref, len_send.at[0], device(0, y, target_of(z), core)).start()

        @pl.when(loops[0])
        def _():
            to = device(X - 1, y, onward[0], core)
            remote(len_ref, len_relay, len_send.at[0], len_recv.at[1], to).start()

        @pl.when(crosses_y)
        def _():
            lens_to_prev(len_ref, len_send.at[0], device(0, y + 1, 0, core)).start()

    own_swap.start()

    row_in_keys = lax.broadcasted_iota(jnp.int32, (1, 4 * GROUP_LEN), 1)
    key_position = (row_in_keys // (2 * GROUP_LEN)) * GROUP_LEN + row_in_keys % GROUP_LEN
    key_neighbour = (row_in_keys // GROUP_LEN) % 2

    def key_live(lens):
        length = jnp.where(
            key_neighbour == 0,
            jnp.broadcast_to(lens[:, 0:1], row_in_keys.shape),
            jnp.broadcast_to(lens[:, 1:2], row_in_keys.shape),
        )
        return key_position < length

    def project(rows, slot, at_row=0):
        into = pl.ds(at_row, rows.shape[0])

        def columns_of(tile, carry):
            at = pl.ds(pl.multiple_of(tile * 256, 256), 256)
            keys_ref[slot, into, at] = jnp.dot(
                rows, kw_ref[:, at], preferred_element_type=jnp.float32
            ).astype(jnp.bfloat16)
            vals_ref[slot, into, at] = jnp.dot(
                rows, vw_ref[:, at], preferred_element_type=jnp.float32
            ).astype(jnp.bfloat16)
            return carry

        lax.fori_loop(0, kw_ref.shape[1] // 256, columns_of, 0)

    def attend(first, count, slot, live):
        heads = [pl.ds(head * HEAD_DIM, HEAD_DIM) for head in range(q_ref.shape[1] // HEAD_DIM)]
        scores = [
            lax.dot_general(
                q_ref[first : first + count, at], keys_ref[slot, :, at],
                (((1,), (1,)), ((), ())), preferred_element_type=jnp.float32,
            )
            for at in heads
        ]
        scores = [jnp.where(live, each * HEAD_DIM ** (-0.5), MASK_FILL) for each in scores]
        most = [jnp.max(each, axis=-1, keepdims=True) for each in scores]
        weights = [jnp.exp(each - top) for each, top in zip(scores, most)]
        totals = [jnp.sum(each, axis=-1, keepdims=True) for each in weights]
        attention = [(each / total).astype(jnp.bfloat16) for each, total in zip(weights, totals)]
        return [
            jnp.dot(each, vals_ref[slot, :, at], preferred_element_type=jnp.float32).astype(jnp.bfloat16)
            for each, at in zip(attention, heads)
        ]

    def own_rows(group):
        return rows_ref[:, group].reshape(4 * GROUP_LEN, rows_ref.shape[-1])

    def step_own_project(group):
        if group == 0:
            kw_in.wait()
            vw_in.wait()
            arrived(rows_ref.at[other], own_recv)
        project(own_rows(group), group)

    def step_own_attend():
        q_in.wait()
        lens = len_ref[...]
        live0, live1 = key_live(lens[0:1]), key_live(lens[1:2])
        row = lax.broadcasted_iota(jnp.int32, (16, HEAD_DIM), 0)
        middle = attend(GROUP_LEN - 16, GROUP_LEN + 16, 0, live0)
        end = attend(2 * GROUP_LEN - 16, 16, 1, live1)
        for head, (mid, last) in enumerate(zip(middle, end)):
            at = pl.ds(head * HEAD_DIM, HEAD_DIM)
            own_out[GROUP_LEN - 16 : 2 * GROUP_LEN - 16, at] = mid[:GROUP_LEN]
            own_out[2 * GROUP_LEN - 16 :, at] = jnp.where(row < 15, mid[GROUP_LEN:], last)

    def own_work(step):
        if step == 0:
            step_own_project(0)
        elif step == 1:
            step_own_project(1)
        elif step == 2:
            step_own_attend()

    def forward(column):
        for j in range(COLUMN_PIECES[column]):
            piece, way = PIECES[column, j], j % 2
            src, send, got = relay_at(0, j), forward_sem.at[0, j], relay_sem.at[0, j]

            @pl.when(direct[way])
            def _():
                arrived(src, got)
                to_prev(piece, src, send, device(0, y, target_of(z), core)).start()

            @pl.when(loops[way])
            def _():
                arrived(src, got)
                to = device(column, y, onward[way], core)
                remote(src, relay_at(1, j), send, relay_sem.at[1, j], to).start()

            @pl.when(crosses_y)
            def _():
                arrived(src, got)
                to_prev(piece, src, send, device(0, y + 1, 0, core)).start()

    def pass_on(column, way):
        to = device(0, y, target_of(passed[way]), core)
        for j in range(way, COLUMN_PIECES[column], 2):
            arrived(relay_at(1, j), relay_sem.at[1, j])
            to_prev(PIECES[column, j], relay_at(1, j), forward_sem.at[1, j], to).start()
        if column == X - 1 and way == 0:
            arrived(len_relay, len_recv.at[1])
            lens_to_prev(len_relay, len_send.at[1], to).start()

    def send_across():
        to = device(x + 1, y, z, core)
        for piece in range(N_PIECES):
            to_prev(piece, last_rows(piece), out_sem.at[piece], to).start()
        lens_to_prev(len_ref, len_send.at[0], to).start()

    @pl.when((x < X - 1) & (z < HALF))
    def _():
        send_across()

    for column in columns:
        if column != X - 1:

            @pl.when(x == column)
            def _():
                forward(column)

    @pl.when((x < X - 1) & (z >= HALF))
    def _():
        send_across()

    for way in (0, 1):
        for column in columns:

            @pl.when((x == column) & passes[way])
            def _():
                pass_on(column, way)

    for step in range(3):
        own_work(step)

    @pl.when(has_prev)
    def _():
        for piece in range(N_PIECES):
            arrived(prev_rows(core, piece), prev_sem.at[piece])
            remote(
                prev_rows(core, piece), prev_rows(core, piece), swap_send.at[piece], swap_recv.at[piece], sibling
            ).start()
        arrived(prev_len, len_recv.at[0])
        half = prev_ref.shape[1]
        project(prev_ref[core], 2, pl.multiple_of(core * half, half))
        for piece in range(N_PIECES):
            arrived(prev_rows(other, piece), swap_recv.at[piece])
        project(prev_ref[other], 2, pl.multiple_of(other * half, half))
        live = key_live(prev_len[1:2])
        row = lax.broadcasted_iota(jnp.int32, (16, HEAD_DIM), 0)
        edge = pl.ds(GROUP_LEN - 16, 16)
        for head, first in enumerate(attend(0, GROUP_LEN, 2, live)):
            at = pl.ds(head * HEAD_DIM, HEAD_DIM)
            out_ref[0, : GROUP_LEN - 16, at] = first[: GROUP_LEN - 16]
            out_ref[0, edge, at] = jnp.where(row < 15, first[GROUP_LEN - 16 :], own_out[edge, at])

    @pl.when(jnp.logical_not(has_prev))
    def _():
        row = lax.broadcasted_iota(jnp.int32, (16, own_out.shape[1]), 0)
        edge = pl.ds(GROUP_LEN - 16, 16)
        out_ref[0, : GROUP_LEN - 16] = jnp.zeros((GROUP_LEN - 16, own_out.shape[1]), jnp.bfloat16)
        out_ref[0, edge] = jnp.where(row < 15, jnp.zeros_like(row, jnp.bfloat16), own_out[edge])

    out_ref[0, GROUP_LEN:] = own_out[GROUP_LEN:]

    left(rows_ref.at[core], own_send)

    @pl.when((x < X - 1) | (z < Z - 1) | (y < X - 1))
    def _():
        for piece in range(N_PIECES):
            left(last_rows(piece), out_sem.at[piece])
        left(len_ref, len_send.at[0])

    for column in columns:
        if column != X - 1:

            @pl.when((x == column) & ((z < Z - 1) | (y < X - 1)))
            def _():
                for j in range(COLUMN_PIECES[column]):
                    left(relay_at(0, j), forward_sem.at[0, j])

        for way in (0, 1):

            @pl.when((x == column) & passes[way])
            def _():
                for j in range(way, COLUMN_PIECES[column], 2):
                    left(relay_at(1, j), forward_sem.at[1, j])
                if column == X - 1 and way == 0:
                    left(len_relay, len_send.at[1])

    @pl.when(has_prev)
    def _():
        for piece in range(N_PIECES):
            left(prev_rows(core, piece), swap_send.at[piece])


def shards(queries, encodings, neighbour_lengths, key_weight, value_weight):
    _, group_count, neighbours, half_rows, enc_width = encodings.shape
    tok_count, col_count = queries.shape[1:]
    bf16 = jnp.bfloat16
    anywhere = pl.BlockSpec(memory_space=pl.ANY)
    dma = pltpu.SemaphoreType.DMA
    return pl.pallas_call(
        kernel,
        out_shape=pltpu.VMEM(queries.shape, bf16),
        in_specs=[anywhere] * 5,
        out_specs=pl.BlockSpec(memory_space=pltpu.VMEM),
        scratch_shapes=[
            pltpu.VMEM((tok_count, col_count), bf16),
            pltpu.VMEM(key_weight.shape, bf16),
            pltpu.VMEM(value_weight.shape, bf16),
            pltpu.VMEM((group_count, neighbours), jnp.int32),
            pltpu.VMEM((group_count, neighbours), jnp.int32),
            pltpu.VMEM((2, group_count, neighbours, half_rows, enc_width), bf16),
            pltpu.VMEM((2, neighbours * half_rows, enc_width), bf16),
            pltpu.VMEM((3, 2 * neighbours * half_rows, col_count), bf16),
            pltpu.VMEM((3, 2 * neighbours * half_rows, col_count), bf16),
            pltpu.VMEM((tok_count, col_count), bf16),
            pltpu.VMEM((2, MOST * PIECE_ROWS, enc_width), bf16),
            pltpu.VMEM((group_count, neighbours), jnp.int32),
            dma((5,)),
            dma((N_PIECES,)),
            dma((2, MOST)),
            dma((2, MOST)),
            dma((N_PIECES,)),
            dma((N_PIECES,)),
            dma((N_PIECES,)),
            dma((2,)),
            dma((2,)),
            dma,
            dma,
        ],
        compiler_params=pltpu.CompilerParams(
            collective_id=0, has_side_effects=True, vmem_limit_bytes=56 * 2**20
        ),
        name="attend_neighbours",
    )(queries, encodings, neighbour_lengths, key_weight, value_weight)


def solution(mesh):
    placed = (
        P(None, ("seq", "fsdp"), "grp"),
        P(None, ("seq", "fsdp"), None, "grp", None),
        P(None, ("seq", "fsdp"), None),
        P(None, "grp"),
        P(None, "grp"),
    )
    return jax.shard_map(
        shards,
        mesh=mesh,
        in_specs=placed,
        out_specs=P(None, ("seq", "fsdp"), "grp"),
        check_vma=False,
    )
```

```python
import jax
import jax.numpy as jnp
from jax import lax
from jax.experimental import pallas as pl
from jax.experimental.pallas import tpu as pltpu
from jax.sharding import PartitionSpec as P

HEAD_DIM = 128
GROUP_LEN = 64
MASK_FILL = -1e30
MESH_ID = pl.DeviceIdType.MESH

X, Z, HALF = 4, 32, 16
COLUMN_PIECES = {3: 4, 0: 4, 2: 4, 1: 4}
HOPS = (((0, 8, 8), (18,26,2)), ((0, 3, -4), (3, 8, 8), (18,26,2)))
PIECE_ROWS = 8
PIECES, SPANS = {}, {}
for _column, _count in COLUMN_PIECES.items():
    SPANS[_column] = (len(PIECES), _count)
    for _j in range(_count):
        PIECES[_column, _j] = len(PIECES)
N_PIECES = len(PIECES)
MOST = max(COLUMN_PIECES.values())


def kernel(
    q_hbm, enc_hbm, len_hbm, kw_hbm, vw_hbm, out_ref,
    q_ref, kw_ref, vw_ref, len_ref, prev_len, rows_ref, prev_ref, keys_ref, vals_ref, own_edge,
    relay, len_relay,
    in_sem, out_sem, relay_sem, forward_sem, prev_sem, swap_send, swap_recv,
    len_send, len_recv, own_send, own_recv,
):
    seq, fsdp, core = lax.axis_index("seq"), lax.axis_index("fsdp"), lax.axis_index("grp")
    x, y = lax.rem(fsdp, X), lax.div(seq, HALF)
    z = lax.rem(seq, HALF) + HALF * lax.div(fsdp, X)
    other = 1 - core

    def device(to_x, to_y, to_z, to_core):
        return (to_y * HALF + lax.rem(to_z, HALF), lax.div(to_z, HALF) * X + to_x, to_core)

    sibling = device(x, y, z, other)
    last_z = (z == Z - 1)
    crosses_y = last_z & (y < X - 1)
    has_prev = (x > 0) | (z > 0) | (y > 0)
    columns = list(COLUMN_PIECES)

    def wrap(at):
        return lax.rem(at + Z, Z)

    def hop_of(origin, way):
        hop = jnp.zeros_like(origin)
        for first, end, by in HOPS[way]:
            hop = jnp.where((origin >= first) & (origin < end), by, hop)
        return hop

    def passed_by(way):
        origin = jnp.full_like(z, Z)
        for first, end, by in HOPS[way]:
            at = wrap(z - by)
            origin = jnp.where((at >= first) & (at < end), at, origin)
        return origin

    hops = [hop_of(z, way) for way in (0, 1)]
    direct = [(hop == 0) & (z < Z - 1) for hop in hops]
    loops = [hop != 0 for hop in hops]
    onward = [wrap(z + hop) for hop in hops]
    passed = [passed_by(way) for way in (0, 1)]
    passes = [origin < Z for origin in passed]

    def target_of(origin):
        return jnp.where(origin < HALF, origin + HALF, origin - (HALF - 1))

    def origin_of(target):
        return jnp.where(target < HALF, target + (HALF - 1), target - HALF)

    def remote(src, dst, send, recv, to):
        return pltpu.make_async_remote_copy(
            src_ref=src, dst_ref=dst, send_sem=send, recv_sem=recv, device_id=to, device_id_type=MESH_ID
        )

    def arrived(dst, recv):
        remote(dst, dst, own_send, recv, sibling).wait_recv()

    def left(src, send):
        remote(src, src, send, own_recv, sibling).wait_send()

    barrier = pltpu.get_barrier_semaphore()

    def greet(who):
        pl.semaphore_signal(barrier, 1, device_id=who, device_id_type=MESH_ID)

    greet(sibling)

    @pl.when(x > 0)
    def _():
        greet(device(x - 1, y, z, core))

    for column in columns:
        if column != X - 1:

            @pl.when(x == column)
            def _():
                greet(device(X - 1, y, z, core))

    on_column = (x == columns[0])
    for column in columns[1:]:
        on_column = on_column | (x == column)

    for way in (0, 1):

        @pl.when(on_column & passes[way])
        def _():
            greet(device(x, y, passed[way], core))

    @pl.when((x == 0) & (z > 0))
    def _():
        origin = origin_of(z)
        for column in columns:
            for way in (0, 1):
                greet(device(column, y, wrap(origin + hop_of(origin, way)), core))

    @pl.when((x == 0) & (z == 0) & (y > 0))
    def _():
        for column in columns:
            greet(device(column, y - 1, Z - 1, core))

    rows_in = pltpu.make_async_copy(enc_hbm.at[0], rows_ref.at[core], in_sem.at[0])
    kw_in = pltpu.make_async_copy(kw_hbm, kw_ref, in_sem.at[1])
    vw_in = pltpu.make_async_copy(vw_hbm, vw_ref, in_sem.at[2])
    q_in = pltpu.make_async_copy(q_hbm.at[0], q_ref, in_sem.at[3])
    len_in = pltpu.make_async_copy(len_hbm.at[0], len_ref, in_sem.at[4])
    for copy in (rows_in, len_in, kw_in, vw_in, q_in):
        copy.start()

    def one(condition, count=1):
        return jnp.where(condition, count, 0)

    peers = 1 + one(x < X - 1) + one(x == X - 1, len(columns) - 1)
    column_peers = one(crosses_y)
    for way in (0, 1):
        column_peers = column_peers + one(z < Z - 1) + one(passes[way])
    pl.semaphore_wait(barrier, peers + jnp.where(on_column, column_peers, 0))

    def last_rows(piece):
        at = piece * PIECE_ROWS
        return rows_ref.at[core, 1, at // GROUP_LEN, pl.ds(at % GROUP_LEN, PIECE_ROWS)]

    def prev_rows(half, piece):
        return prev_ref.at[half, pl.ds(piece * PIECE_ROWS, PIECE_ROWS)]

    def span_rows(half, column):
        first, count = SPANS[column]
        return prev_ref.at[half, pl.ds(first * PIECE_ROWS, count * PIECE_ROWS)]

    def to_prev(piece, src, send, to):
        return remote(src, prev_rows(core, piece), send, prev_sem.at[piece], to)

    def relay_at(stage, j):
        return relay.at[stage, pl.ds(j * PIECE_ROWS, PIECE_ROWS)]

    def lens_to_prev(src, send, to):
        return remote(src, prev_len, send, len_recv.at[0], to)

    rows_in.wait()
    len_in.wait()
    own_swap = remote(rows_ref.at[core], rows_ref.at[core], own_send, own_recv, sibling)

    @pl.when(x == X - 1)
    def _():
        for (column, j), piece in PIECES.items():
            src, send, way = last_rows(piece), out_sem.at[piece], j % 2
            if column != X - 1:

                @pl.when((z < Z - 1) | (y < X - 1))
                def _():
                    to = device(column, y, z, core)
                    remote(src, relay_at(0, j), send, relay_sem.at[0, j], to).start()

            else:

                @pl.when(direct[way])
                def _():
                    to_prev(piece, src, send, device(0, y, target_of(z), core)).start()

                @pl.when(loops[way])
                def _():
                    to = device(column, y, onward[way], core)
                    remote(src, relay_at(1, j), send, relay_sem.at[1, j], to).start()

                @pl.when(crosses_y)
                def _():
                    to_prev(piece, src, send, device(0, y + 1, 0, core)).start()

        @pl.when(direct[0])
        def _():
            lens_to_prev(len_ref, len_send.at[0], device(0, y, target_of(z), core)).start()

        @pl.when(loops[0])
        def _():
            to = device(X - 1, y, onward[0], core)
            remote(len_ref, len_relay, len_send.at[0], len_recv.at[1], to).start()

        @pl.when(crosses_y)
        def _():
            lens_to_prev(len_ref, len_send.at[0], device(0, y + 1, 0, core)).start()

    own_swap.start()

    row_in_keys = lax.broadcasted_iota(jnp.int32, (1, 4 * GROUP_LEN), 1)
    key_position = (row_in_keys // (2 * GROUP_LEN)) * GROUP_LEN + row_in_keys % GROUP_LEN
    key_neighbour = (row_in_keys // GROUP_LEN) % 2

    def key_live(lens):
        length = jnp.where(
            key_neighbour == 0,
            jnp.broadcast_to(lens[:, 0:1], row_in_keys.shape),
            jnp.broadcast_to(lens[:, 1:2], row_in_keys.shape),
        )
        return key_position < length

    def project(rows, slot, at_row=0):
        into = pl.ds(at_row, rows.shape[0])

        for tile in range(kw_ref.shape[1] // 256):
            at = pl.ds(tile * 256, 256)
            keys_ref[slot, into, at] = jnp.dot(
                rows, kw_ref[:, at], preferred_element_type=jnp.float32
            ).astype(jnp.bfloat16)
            vals_ref[slot, into, at] = jnp.dot(
                rows, vw_ref[:, at], preferred_element_type=jnp.float32
            ).astype(jnp.bfloat16)

    def attend(first, count, slot, live):
        heads = [pl.ds(head * HEAD_DIM, HEAD_DIM) for head in range(q_ref.shape[1] // HEAD_DIM)]
        scores = [
            lax.dot_general(
                q_ref[first : first + count, at], keys_ref[slot, :, at],
                (((1,), (1,)), ((), ())), preferred_element_type=jnp.float32,
            )
            for at in heads
        ]
        scores = [jnp.where(live, each * HEAD_DIM ** (-0.5), MASK_FILL) for each in scores]
        most = [jnp.max(each, axis=-1, keepdims=True) for each in scores]
        weights = [jnp.exp(each - top) for each, top in zip(scores, most)]
        totals = [jnp.sum(each, axis=-1, keepdims=True) for each in weights]
        attention = [(each / total).astype(jnp.bfloat16) for each, total in zip(weights, totals)]
        return [
            jnp.dot(each, vals_ref[slot, :, at], preferred_element_type=jnp.float32).astype(jnp.bfloat16)
            for each, at in zip(attention, heads)
        ]

    def own_rows(group):
        return rows_ref[:, group].reshape(4 * GROUP_LEN, rows_ref.shape[-1])

    def step_own_project(group):
        if group == 0:
            kw_in.wait()
            vw_in.wait()
            arrived(rows_ref.at[other], own_recv)
        project(own_rows(group), group)

    def step_own_attend():
        q_in.wait()
        lens = len_ref[...]
        live0, live1 = key_live(lens[0:1]), key_live(lens[1:2])
        row = lax.broadcasted_iota(jnp.int32, (16, HEAD_DIM), 0)
        middle = attend(GROUP_LEN - 16, GROUP_LEN + 16, 0, live0)
        end = attend(2 * GROUP_LEN - 16, 16, 1, live1)
        for head, (mid, last) in enumerate(zip(middle, end)):
            at = pl.ds(head * HEAD_DIM, HEAD_DIM)
            own_edge[:, at] = mid[:16]
            out_ref[0, GROUP_LEN : 2 * GROUP_LEN - 16, at] = mid[16:GROUP_LEN]
            out_ref[0, 2 * GROUP_LEN - 16 :, at] = jnp.where(row < 15, mid[GROUP_LEN:], last)

    def own_work(step):
        if step == 0:
            step_own_project(0)
        elif step == 1:
            step_own_project(1)
        elif step == 2:
            step_own_attend()

    def forward(column):
        for j in range(COLUMN_PIECES[column]):
            piece, way = PIECES[column, j], j % 2
            src, send, got = relay_at(0, j), forward_sem.at[0, j], relay_sem.at[0, j]

            @pl.when(direct[way])
            def _():
                arrived(src, got)
                to_prev(piece, src, send, device(0, y, target_of(z), core)).start()

            @pl.when(loops[way])
            def _():
                arrived(src, got)
                to = device(column, y, onward[way], core)
                remote(src, relay_at(1, j), send, relay_sem.at[1, j], to).start()

            @pl.when(crosses_y)
            def _():
                arrived(src, got)
                to_prev(piece, src, send, device(0, y + 1, 0, core)).start()

    def pass_on(column, way):
        to = device(0, y, target_of(passed[way]), core)
        for j in range(way, COLUMN_PIECES[column], 2):
            arrived(relay_at(1, j), relay_sem.at[1, j])
            to_prev(PIECES[column, j], relay_at(1, j), forward_sem.at[1, j], to).start()
        if column == X - 1 and way == 0:
            arrived(len_relay, len_recv.at[1])
            lens_to_prev(len_relay, len_send.at[1], to).start()

    def send_across():
        to = device(x + 1, y, z, core)
        for piece in range(N_PIECES):
            to_prev(piece, last_rows(piece), out_sem.at[piece], to).start()
        lens_to_prev(len_ref, len_send.at[0], to).start()

    @pl.when((x < X - 1) & (z < HALF))
    def _():
        send_across()

    for column in columns:
        if column != X - 1:

            @pl.when(x == column)
            def _():
                forward(column)

    @pl.when((x < X - 1) & (z >= HALF))
    def _():
        send_across()

    for way in (0, 1):
        for column in columns:

            @pl.when((x == column) & passes[way])
            def _():
                pass_on(column, way)

    for step in range(3):
        own_work(step)

    left(rows_ref.at[core], own_send)

    @pl.when((x < X - 1) | (z < Z - 1) | (y < X - 1))
    def _():
        for piece in range(N_PIECES):
            left(last_rows(piece), out_sem.at[piece])
        left(len_ref, len_send.at[0])

    for column in columns:
        if column != X - 1:

            @pl.when((x == column) & ((z < Z - 1) | (y < X - 1)))
            def _():
                for j in range(COLUMN_PIECES[column]):
                    left(relay_at(0, j), forward_sem.at[0, j])

        for way in (0, 1):

            @pl.when((x == column) & passes[way])
            def _():
                for j in range(way, COLUMN_PIECES[column], 2):
                    left(relay_at(1, j), forward_sem.at[1, j])
                if column == X - 1 and way == 0:
                    left(len_relay, len_send.at[1])

    @pl.when(has_prev)
    def _():
        for index, column in enumerate(columns):
            for j in range(COLUMN_PIECES[column]):
                piece = PIECES[column, j]
                arrived(prev_rows(core, piece), prev_sem.at[piece])
            span = span_rows(core, column)
            remote(span, span, swap_send.at[index], swap_recv.at[index], sibling).start()
        arrived(prev_len, len_recv.at[0])
        half = prev_ref.shape[1]
        project(prev_ref[core], 2, pl.multiple_of(core * half, half))
        for index, column in enumerate(columns):
            arrived(span_rows(other, column), swap_recv.at[index])
        project(prev_ref[other], 2, pl.multiple_of(other * half, half))
        live = key_live(prev_len[1:2])
        row = lax.broadcasted_iota(jnp.int32, (16, HEAD_DIM), 0)
        edge = pl.ds(GROUP_LEN - 16, 16)
        for head, first in enumerate(attend(0, GROUP_LEN, 2, live)):
            at = pl.ds(head * HEAD_DIM, HEAD_DIM)
            out_ref[0, : GROUP_LEN - 16, at] = first[: GROUP_LEN - 16]
            out_ref[0, edge, at] = jnp.where(row < 15, first[GROUP_LEN - 16 :], own_edge[:, at])

    @pl.when(jnp.logical_not(has_prev))
    def _():
        row = lax.broadcasted_iota(jnp.int32, own_edge.shape, 0)
        out_ref[0, : GROUP_LEN - 16] = jnp.zeros((GROUP_LEN - 16, own_edge.shape[1]), jnp.bfloat16)
        edge = pl.ds(GROUP_LEN - 16, 16)
        out_ref[0, edge] = jnp.where(row < 15, jnp.zeros_like(row, jnp.bfloat16), own_edge[...])

    @pl.when(has_prev)
    def _():
        for index, column in enumerate(columns):
            left(span_rows(core, column), swap_send.at[index])


def shards(queries, encodings, neighbour_lengths, key_weight, value_weight):
    _, group_count, neighbours, half_rows, enc_width = encodings.shape
    tok_count, col_count = queries.shape[1:]
    bf16 = jnp.bfloat16
    anywhere = pl.BlockSpec(memory_space=pl.ANY)
    dma = pltpu.SemaphoreType.DMA
    return pl.pallas_call(
        kernel,
        out_shape=pltpu.VMEM(queries.shape, bf16),
        in_specs=[anywhere] * 5,
        out_specs=pl.BlockSpec(memory_space=pltpu.VMEM),
        scratch_shapes=[
            pltpu.VMEM((tok_count, col_count), bf16),
            pltpu.VMEM(key_weight.shape, bf16),
            pltpu.VMEM(value_weight.shape, bf16),
            pltpu.VMEM((group_count, neighbours), jnp.int32),
            pltpu.VMEM((group_count, neighbours), jnp.int32),
            pltpu.VMEM((2, group_count, neighbours, half_rows, enc_width), bf16),
            pltpu.VMEM((2, neighbours * half_rows, enc_width), bf16),
            pltpu.VMEM((3, 2 * neighbours * half_rows, col_count), bf16),
            pltpu.VMEM((3, 2 * neighbours * half_rows, col_count), bf16),
            pltpu.VMEM((16, col_count), bf16),
            pltpu.VMEM((2, MOST * PIECE_ROWS, enc_width), bf16),
            pltpu.VMEM((group_count, neighbours), jnp.int32),
            dma((5,)),
            dma((N_PIECES,)),
            dma((2, MOST)),
            dma((2, MOST)),
            dma((N_PIECES,)),
            dma((len(COLUMN_PIECES),)),
            dma((len(COLUMN_PIECES),)),
            dma((2,)),
            dma((2,)),
            dma,
            dma,
        ],
        compiler_params=pltpu.CompilerParams(
            collective_id=0, has_side_effects=True, vmem_limit_bytes=56 * 2**20
        ),
        name="attend_neighbours",
    )(queries, encodings, neighbour_lengths, key_weight, value_weight)


def solution(mesh):
    placed = (
        P(None, ("seq", "fsdp"), "grp"),
        P(None, ("seq", "fsdp"), None, "grp", None),
        P(None, ("seq", "fsdp"), None),
        P(None, "grp"),
        P(None, "grp"),
    )
    return jax.shard_map(
        shards,
        mesh=mesh,
        in_specs=placed,
        out_specs=P(None, ("seq", "fsdp"), "grp"),
        check_vma=False,
    )
```

```python
import jax
import jax.numpy as jnp
from jax import lax
from jax.experimental import pallas as pl
from jax.experimental.pallas import tpu as pltpu
from jax.sharding import PartitionSpec as P

HEAD_DIM = 128
GROUP_LEN = 64
MASK_FILL = -1e30
MESH_ID = pl.DeviceIdType.MESH

X, Z, HALF = 4, 32, 16
COLUMN_PIECES = {3: 4, 0: 4, 2: 4, 1: 4}
HOPS = (((0, 6, 8), (12, 13, -5), (19, 24, 2)), ((0, 3, -4), (3, 6, 8), (12, 13, -5), (19, 24, 2)))
PIECE_ROWS = 8
PIECES, SPANS = {}, {}
for _column, _count in COLUMN_PIECES.items():
    SPANS[_column] = (len(PIECES), _count)
    for _j in range(_count):
        PIECES[_column, _j] = len(PIECES)
N_PIECES = len(PIECES)
MOST = max(COLUMN_PIECES.values())


def kernel(
    q_hbm, enc_hbm, len_hbm, kw_hbm, vw_hbm, out_ref,
    q_ref, kw_ref, vw_ref, len_ref, prev_len, rows_ref, prev_ref, keys_ref, vals_ref, own_edge,
    relay, len_relay,
    in_sem, out_sem, relay_sem, forward_sem, prev_sem, swap_send, swap_recv,
    len_send, len_recv, own_send, own_recv,
):
    seq, fsdp, core = lax.axis_index("seq"), lax.axis_index("fsdp"), lax.axis_index("grp")
    x, y = lax.rem(fsdp, X), lax.div(seq, HALF)
    z = lax.rem(seq, HALF) + HALF * lax.div(fsdp, X)
    other = 1 - core

    def device(to_x, to_y, to_z, to_core):
        return (to_y * HALF + lax.rem(to_z, HALF), lax.div(to_z, HALF) * X + to_x, to_core)

    sibling = device(x, y, z, other)
    last_z = (z == Z - 1)
    crosses_y = last_z & (y < X - 1)
    has_prev = (x > 0) | (z > 0) | (y > 0)
    columns = list(COLUMN_PIECES)

    def wrap(at):
        return lax.rem(at + Z, Z)

    def hop_of(origin, way):
        hop = jnp.zeros_like(origin)
        for first, end, by in HOPS[way]:
            hop = jnp.where((origin >= first) & (origin < end), by, hop)
        return hop

    def passed_by(way):
        origin = jnp.full_like(z, Z)
        for first, end, by in HOPS[way]:
            at = wrap(z - by)
            origin = jnp.where((at >= first) & (at < end), at, origin)
        return origin

    hops = [hop_of(z, way) for way in (0, 1)]
    direct = [(hop == 0) & (z < Z - 1) for hop in hops]
    loops = [hop != 0 for hop in hops]
    onward = [wrap(z + hop) for hop in hops]
    passed = [passed_by(way) for way in (0, 1)]
    passes = [origin < Z for origin in passed]

    def target_of(origin):
        return jnp.where(origin < HALF, origin + HALF, origin - (HALF - 1))

    def origin_of(target):
        return jnp.where(target < HALF, target + (HALF - 1), target - HALF)

    def remote(src, dst, send, recv, to):
        return pltpu.make_async_remote_copy(
            src_ref=src, dst_ref=dst, send_sem=send, recv_sem=recv, device_id=to, device_id_type=MESH_ID
        )

    def arrived(dst, recv):
        remote(dst, dst, own_send, recv, sibling).wait_recv()

    def left(src, send):
        remote(src, src, send, own_recv, sibling).wait_send()

    barrier = pltpu.get_barrier_semaphore()

    def greet(who):
        pl.semaphore_signal(barrier, 1, device_id=who, device_id_type=MESH_ID)

    greet(sibling)

    @pl.when(x > 0)
    def _():
        greet(device(x - 1, y, z, core))

    for column in columns:
        if column != X - 1:

            @pl.when(x == column)
            def _():
                greet(device(X - 1, y, z, core))

    on_column = (x == columns[0])
    for column in columns[1:]:
        on_column = on_column | (x == column)

    for way in (0, 1):

        @pl.when(on_column & passes[way])
        def _():
            greet(device(x, y, passed[way], core))

    @pl.when((x == 0) & (z > 0))
    def _():
        origin = origin_of(z)
        for column in columns:
            for way in (0, 1):
                greet(device(column, y, wrap(origin + hop_of(origin, way)), core))

    @pl.when((x == 0) & (z == 0) & (y > 0))
    def _():
        for column in columns:
            greet(device(column, y - 1, Z - 1, core))

    rows_in = pltpu.make_async_copy(enc_hbm.at[0], rows_ref.at[core], in_sem.at[0])
    kw_in = pltpu.make_async_copy(kw_hbm, kw_ref, in_sem.at[1])
    vw_in = pltpu.make_async_copy(vw_hbm, vw_ref, in_sem.at[2])
    q_in = pltpu.make_async_copy(q_hbm.at[0], q_ref, in_sem.at[3])
    len_in = pltpu.make_async_copy(len_hbm.at[0], len_ref, in_sem.at[4])
    for copy in (rows_in, len_in, kw_in, vw_in, q_in):
        copy.start()

    def one(condition, count=1):
        return jnp.where(condition, count, 0)

    peers = 1 + one(x < X - 1) + one(x == X - 1, len(columns) - 1)
    column_peers = one(crosses_y)
    for way in (0, 1):
        column_peers = column_peers + one(z < Z - 1) + one(passes[way])
    pl.semaphore_wait(barrier, peers + jnp.where(on_column, column_peers, 0))

    def last_rows(piece):
        at = piece * PIECE_ROWS
        return rows_ref.at[core, 1, at // GROUP_LEN, pl.ds(at % GROUP_LEN, PIECE_ROWS)]

    def prev_rows(half, piece):
        return prev_ref.at[half, pl.ds(piece * PIECE_ROWS, PIECE_ROWS)]

    def span_rows(half, column):
        first, count = SPANS[column]
        return prev_ref.at[half, pl.ds(first * PIECE_ROWS, count * PIECE_ROWS)]

    def to_prev(piece, src, send, to):
        return remote(src, prev_rows(core, piece), send, prev_sem.at[piece], to)

    def relay_at(stage, j):
        return relay.at[stage, pl.ds(j * PIECE_ROWS, PIECE_ROWS)]

    def lens_to_prev(src, send, to):
        return remote(src, prev_len, send, len_recv.at[0], to)

    rows_in.wait()
    len_in.wait()
    own_swap = remote(rows_ref.at[core], rows_ref.at[core], own_send, own_recv, sibling)

    @pl.when(x == X - 1)
    def _():
        for (column, j), piece in PIECES.items():
            src, send, way = last_rows(piece), out_sem.at[piece], j % 2
            if column != X - 1:

                @pl.when((z < Z - 1) | (y < X - 1))
                def _():
                    to = device(column, y, z, core)
                    remote(src, relay_at(0, j), send, relay_sem.at[0, j], to).start()

            else:

                @pl.when(direct[way])
                def _():
                    to_prev(piece, src, send, device(0, y, target_of(z), core)).start()

                @pl.when(loops[way])
                def _():
                    to = device(column, y, onward[way], core)
                    remote(src, relay_at(1, j), send, relay_sem.at[1, j], to).start()

                @pl.when(crosses_y)
                def _():
                    to_prev(piece, src, send, device(0, y + 1, 0, core)).start()

        @pl.when(direct[0])
        def _():
            lens_to_prev(len_ref, len_send.at[0], device(0, y, target_of(z), core)).start()

        @pl.when(loops[0])
        def _():
            to = device(X - 1, y, onward[0], core)
            remote(len_ref, len_relay, len_send.at[0], len_recv.at[1], to).start()

        @pl.when(crosses_y)
        def _():
            lens_to_prev(len_ref, len_send.at[0], device(0, y + 1, 0, core)).start()

    own_swap.start()

    row_in_keys = lax.broadcasted_iota(jnp.int32, (1, 4 * GROUP_LEN), 1)
    key_position = (row_in_keys // (2 * GROUP_LEN)) * GROUP_LEN + row_in_keys % GROUP_LEN
    key_neighbour = (row_in_keys // GROUP_LEN) % 2

    def key_live(lens):
        length = jnp.where(
            key_neighbour == 0,
            jnp.broadcast_to(lens[:, 0:1], row_in_keys.shape),
            jnp.broadcast_to(lens[:, 1:2], row_in_keys.shape),
        )
        return key_position < length

    def project(rows, slot, at_row=0):
        into = pl.ds(at_row, rows.shape[0])

        for tile in range(kw_ref.shape[1] // 256):
            at = pl.ds(tile * 256, 256)
            keys_ref[slot, into, at] = jnp.dot(
                rows, kw_ref[:, at], preferred_element_type=jnp.float32
            ).astype(jnp.bfloat16)
            vals_ref[slot, into, at] = jnp.dot(
                rows, vw_ref[:, at], preferred_element_type=jnp.float32
            ).astype(jnp.bfloat16)

    def attend(first, count, slot, live):
        heads = [pl.ds(head * HEAD_DIM, HEAD_DIM) for head in range(q_ref.shape[1] // HEAD_DIM)]
        scores = [
            lax.dot_general(
                q_ref[first : first + count, at], keys_ref[slot, :, at],
                (((1,), (1,)), ((), ())), preferred_element_type=jnp.float32,
            )
            for at in heads
        ]
        scores = [jnp.where(live, each * HEAD_DIM ** (-0.5), MASK_FILL) for each in scores]
        most = [jnp.max(each, axis=-1, keepdims=True) for each in scores]
        weights = [jnp.exp(each - top) for each, top in zip(scores, most)]
        totals = [jnp.sum(each, axis=-1, keepdims=True) for each in weights]
        attention = [(each / total).astype(jnp.bfloat16) for each, total in zip(weights, totals)]
        return [
            jnp.dot(each, vals_ref[slot, :, at], preferred_element_type=jnp.float32).astype(jnp.bfloat16)
            for each, at in zip(attention, heads)
        ]

    def own_rows(group):
        return rows_ref[:, group].reshape(4 * GROUP_LEN, rows_ref.shape[-1])

    def step_own_project(group):
        if group == 0:
            kw_in.wait()
            vw_in.wait()
            arrived(rows_ref.at[other], own_recv)
        project(own_rows(group), group)

    def step_own_attend():
        q_in.wait()
        lens = len_ref[...]
        live0, live1 = key_live(lens[0:1]), key_live(lens[1:2])
        row = lax.broadcasted_iota(jnp.int32, (16, HEAD_DIM), 0)
        middle = attend(GROUP_LEN - 16, GROUP_LEN + 16, 0, live0)
        end = attend(2 * GROUP_LEN - 16, 16, 1, live1)
        for head, (mid, last) in enumerate(zip(middle, end)):
            at = pl.ds(head * HEAD_DIM, HEAD_DIM)
            own_edge[:, at] = mid[:16]
            out_ref[0, GROUP_LEN : 2 * GROUP_LEN - 16, at] = mid[16:GROUP_LEN]
            out_ref[0, 2 * GROUP_LEN - 16 :, at] = jnp.where(row < 15, mid[GROUP_LEN:], last)

    def own_work(step):
        if step == 0:
            step_own_project(0)
        elif step == 1:
            step_own_project(1)
        elif step == 2:
            step_own_attend()

    def forward(column):
        for j in range(COLUMN_PIECES[column]):
            piece, way = PIECES[column, j], j % 2
            src, send, got = relay_at(0, j), forward_sem.at[0, j], relay_sem.at[0, j]

            @pl.when(direct[way])
            def _():
                arrived(src, got)
                to_prev(piece, src, send, device(0, y, target_of(z), core)).start()

            @pl.when(loops[way])
            def _():
                arrived(src, got)
                to = device(column, y, onward[way], core)
                remote(src, relay_at(1, j), send, relay_sem.at[1, j], to).start()

            @pl.when(crosses_y)
            def _():
                arrived(src, got)
                to_prev(piece, src, send, device(0, y + 1, 0, core)).start()

    def pass_on(column, way):
        to = device(0, y, target_of(passed[way]), core)
        for j in range(way, COLUMN_PIECES[column], 2):
            arrived(relay_at(1, j), relay_sem.at[1, j])
            to_prev(PIECES[column, j], relay_at(1, j), forward_sem.at[1, j], to).start()
        if column == X - 1 and way == 0:
            arrived(len_relay, len_recv.at[1])
            lens_to_prev(len_relay, len_send.at[1], to).start()

    def send_across():
        to = device(x + 1, y, z, core)
        for piece in range(N_PIECES):
            to_prev(piece, last_rows(piece), out_sem.at[piece], to).start()
        lens_to_prev(len_ref, len_send.at[0], to).start()

    @pl.when((x < X - 1) & (z < HALF))
    def _():
        send_across()

    for column in columns:
        if column != X - 1:

            @pl.when(x == column)
            def _():
                forward(column)

    @pl.when((x < X - 1) & (z >= HALF))
    def _():
        send_across()

    for way in (0, 1):
        for column in columns:

            @pl.when((x == column) & passes[way])
            def _():
                pass_on(column, way)

    for step in range(3):
        own_work(step)

    left(rows_ref.at[core], own_send)

    @pl.when((x < X - 1) | (z < Z - 1) | (y < X - 1))
    def _():
        for piece in range(N_PIECES):
            left(last_rows(piece), out_sem.at[piece])
        left(len_ref, len_send.at[0])

    for column in columns:
        if column != X - 1:

            @pl.when((x == column) & ((z < Z - 1) | (y < X - 1)))
            def _():
                for j in range(COLUMN_PIECES[column]):
                    left(relay_at(0, j), forward_sem.at[0, j])

        for way in (0, 1):

            @pl.when((x == column) & passes[way])
            def _():
                for j in range(way, COLUMN_PIECES[column], 2):
                    left(relay_at(1, j), forward_sem.at[1, j])
                if column == X - 1 and way == 0:
                    left(len_relay, len_send.at[1])

    @pl.when(has_prev)
    def _():
        for index, column in enumerate(columns):
            for j in range(COLUMN_PIECES[column]):
                piece = PIECES[column, j]
                arrived(prev_rows(core, piece), prev_sem.at[piece])
            span = span_rows(core, column)
            remote(span, span, swap_send.at[index], swap_recv.at[index], sibling).start()
        arrived(prev_len, len_recv.at[0])
        half = prev_ref.shape[1]
        project(prev_ref[core], 2, pl.multiple_of(core * half, half))
        for index, column in enumerate(columns):
            arrived(span_rows(other, column), swap_recv.at[index])
        project(prev_ref[other], 2, pl.multiple_of(other * half, half))
        live = key_live(prev_len[1:2])
        row = lax.broadcasted_iota(jnp.int32, (16, HEAD_DIM), 0)
        edge = pl.ds(GROUP_LEN - 16, 16)
        for head, first in enumerate(attend(0, GROUP_LEN, 2, live)):
            at = pl.ds(head * HEAD_DIM, HEAD_DIM)
            out_ref[0, : GROUP_LEN - 16, at] = first[: GROUP_LEN - 16]
            out_ref[0, edge, at] = jnp.where(row < 15, first[GROUP_LEN - 16 :], own_edge[:, at])

    @pl.when(jnp.logical_not(has_prev))
    def _():
        row = lax.broadcasted_iota(jnp.int32, own_edge.shape, 0)
        out_ref[0, : GROUP_LEN - 16] = jnp.zeros((GROUP_LEN - 16, own_edge.shape[1]), jnp.bfloat16)
        edge = pl.ds(GROUP_LEN - 16, 16)
        out_ref[0, edge] = jnp.where(row < 15, jnp.zeros_like(row, jnp.bfloat16), own_edge[...])

    @pl.when(has_prev)
    def _():
        for index, column in enumerate(columns):
            left(span_rows(core, column), swap_send.at[index])


def shards(queries, encodings, neighbour_lengths, key_weight, value_weight):
    _, group_count, neighbours, half_rows, enc_width = encodings.shape
    tok_count, col_count = queries.shape[1:]
    bf16 = jnp.bfloat16
    anywhere = pl.BlockSpec(memory_space=pl.ANY)
    dma = pltpu.SemaphoreType.DMA
    return pl.pallas_call(
        kernel,
        out_shape=pltpu.VMEM(queries.shape, bf16),
        in_specs=[anywhere] * 5,
        out_specs=pl.BlockSpec(memory_space=pltpu.VMEM),
        scratch_shapes=[
            pltpu.VMEM((tok_count, col_count), bf16),
            pltpu.VMEM(key_weight.shape, bf16),
            pltpu.VMEM(value_weight.shape, bf16),
            pltpu.VMEM((group_count, neighbours), jnp.int32),
            pltpu.VMEM((group_count, neighbours), jnp.int32),
            pltpu.VMEM((2, group_count, neighbours, half_rows, enc_width), bf16),
            pltpu.VMEM((2, neighbours * half_rows, enc_width), bf16),
            pltpu.VMEM((3, 2 * neighbours * half_rows, col_count), bf16),
            pltpu.VMEM((3, 2 * neighbours * half_rows, col_count), bf16),
            pltpu.VMEM((16, col_count), bf16),
            pltpu.VMEM((2, MOST * PIECE_ROWS, enc_width), bf16),
            pltpu.VMEM((group_count, neighbours), jnp.int32),
            dma((5,)),
            dma((N_PIECES,)),
            dma((2, MOST)),
            dma((2, MOST)),
            dma((N_PIECES,)),
            dma((len(COLUMN_PIECES),)),
            dma((len(COLUMN_PIECES),)),
            dma((2,)),
            dma((2,)),
            dma,
            dma,
        ],
        compiler_params=pltpu.CompilerParams(
            collective_id=0, has_side_effects=True, vmem_limit_bytes=56 * 2**20
        ),
        name="attend_neighbours",
    )(queries, encodings, neighbour_lengths, key_weight, value_weight)


def solution(mesh):
    placed = (
        P(None, ("seq", "fsdp"), "grp"),
        P(None, ("seq", "fsdp"), None, "grp", None),
        P(None, ("seq", "fsdp"), None),
        P(None, "grp"),
        P(None, "grp"),
    )
    return jax.shard_map(
        shards,
        mesh=mesh,
        in_specs=placed,
        out_specs=P(None, ("seq", "fsdp"), "grp"),
        check_vma=False,
    )
```

```python
import jax
import jax.numpy as jnp
from jax import lax
from jax.experimental import pallas as pl
from jax.experimental.pallas import tpu as pltpu
from jax.sharding import PartitionSpec as P

HEAD_DIM = 128
GROUP_LEN = 64
MASK_FILL = -1e30
MESH_ID = pl.DeviceIdType.MESH

X, Z, HALF = 4, 32, 16
COLUMN_PIECES = {3: 4, 0: 4, 2: 4, 1: 4}
HOPS = (((0, 6, 8), (12, 13, -5), (19, 24, 2)), ((0, 3, -4), (3, 6, 8), (12, 13, -5), (19, 24, 2)))
PIECE_ROWS = 8
PIECES, SPANS = {}, {}
for _column, _count in COLUMN_PIECES.items():
    SPANS[_column] = (len(PIECES), _count)
    for _j in range(_count):
        PIECES[_column, _j] = len(PIECES)
N_PIECES = len(PIECES)
MOST = max(COLUMN_PIECES.values())


def kernel(
    q_hbm, enc_hbm, len_hbm, kw_hbm, vw_hbm, out_ref,
    q_ref, kw_ref, vw_ref, len_ref, prev_len, rows_ref, prev_ref, keys_ref, vals_ref, own_edge,
    relay, len_relay,
    in_sem, out_sem, relay_sem, forward_sem, prev_sem, swap_send, swap_recv,
    len_send, len_recv, own_send, own_recv,
):
    seq, fsdp, core = lax.axis_index("seq"), lax.axis_index("fsdp"), lax.axis_index("grp")
    x, y = lax.rem(fsdp, X), lax.div(seq, HALF)
    z = lax.rem(seq, HALF) + HALF * lax.div(fsdp, X)
    other = 1 - core

    def device(to_x, to_y, to_z, to_core):
        return (to_y * HALF + lax.rem(to_z, HALF), lax.div(to_z, HALF) * X + to_x, to_core)

    sibling = device(x, y, z, other)
    last_z = (z == Z - 1)
    crosses_y = last_z & (y < X - 1)
    has_prev = (x > 0) | (z > 0) | (y > 0)
    columns = list(COLUMN_PIECES)

    def wrap(at):
        return lax.rem(at + Z, Z)

    def hop_of(origin, way):
        hop = jnp.zeros_like(origin)
        for first, end, by in HOPS[way]:
            hop = jnp.where((origin >= first) & (origin < end), by, hop)
        return hop

    def passed_by(way):
        origin = jnp.full_like(z, Z)
        for first, end, by in HOPS[way]:
            at = wrap(z - by)
            origin = jnp.where((at >= first) & (at < end), at, origin)
        return origin

    hops = [hop_of(z, way) for way in (0, 1)]
    direct = [(hop == 0) & (z < Z - 1) for hop in hops]
    loops = [hop != 0 for hop in hops]
    onward = [wrap(z + hop) for hop in hops]
    passed = [passed_by(way) for way in (0, 1)]
    passes = [origin < Z for origin in passed]

    def target_of(origin):
        return jnp.where(origin < HALF, origin + HALF, origin - (HALF - 1))

    def origin_of(target):
        return jnp.where(target < HALF, target + (HALF - 1), target - HALF)

    def remote(src, dst, send, recv, to):
        return pltpu.make_async_remote_copy(
            src_ref=src, dst_ref=dst, send_sem=send, recv_sem=recv, device_id=to, device_id_type=MESH_ID
        )

    def arrived(dst, recv):
        remote(dst, dst, own_send, recv, sibling).wait_recv()

    def left(src, send):
        remote(src, src, send, own_recv, sibling).wait_send()

    barrier = pltpu.get_barrier_semaphore()

    def greet(who):
        pl.semaphore_signal(barrier, 1, device_id=who, device_id_type=MESH_ID)

    greet(sibling)

    @pl.when(x > 0)
    def _():
        greet(device(x - 1, y, z, core))

    for column in columns:
        if column != X - 1:

            @pl.when(x == column)
            def _():
                greet(device(X - 1, y, z, core))

    on_column = (x == columns[0])
    for column in columns[1:]:
        on_column = on_column | (x == column)

    for way in (0, 1):

        @pl.when(on_column & passes[way])
        def _():
            greet(device(x, y, passed[way], core))

    @pl.when((x == 0) & (z > 0))
    def _():
        origin = origin_of(z)
        for column in columns:
            for way in (0, 1):
                greet(device(column, y, wrap(origin + hop_of(origin, way)), core))

    @pl.when((x == 0) & (z == 0) & (y > 0))
    def _():
        for column in columns:
            greet(device(column, y - 1, Z - 1, core))

    rows_in = pltpu.make_async_copy(enc_hbm.at[0], rows_ref.at[core], in_sem.at[0])
    kw_in = pltpu.make_async_copy(kw_hbm, kw_ref, in_sem.at[1])
    vw_in = pltpu.make_async_copy(vw_hbm, vw_ref, in_sem.at[2])
    q_in = pltpu.make_async_copy(q_hbm.at[0], q_ref, in_sem.at[3])
    len_in = pltpu.make_async_copy(len_hbm.at[0], len_ref, in_sem.at[4])
    for copy in (rows_in, len_in, kw_in, vw_in, q_in):
        copy.start()

    def one(condition, count=1):
        return jnp.where(condition, count, 0)

    peers = 1 + one(x < X - 1) + one(x == X - 1, len(columns) - 1)
    column_peers = one(crosses_y)
    for way in (0, 1):
        column_peers = column_peers + one(z < Z - 1) + one(passes[way])
    pl.semaphore_wait(barrier, peers + jnp.where(on_column, column_peers, 0))

    def last_rows(piece):
        at = piece * PIECE_ROWS
        return rows_ref.at[core, 1, at // GROUP_LEN, pl.ds(at % GROUP_LEN, PIECE_ROWS)]

    def prev_rows(half, piece):
        return prev_ref.at[half, pl.ds(piece * PIECE_ROWS, PIECE_ROWS)]

    def span_rows(half, column):
        first, count = SPANS[column]
        return prev_ref.at[half, pl.ds(first * PIECE_ROWS, count * PIECE_ROWS)]

    def to_prev(piece, src, send, to):
        return remote(src, prev_rows(core, piece), send, prev_sem.at[piece], to)

    def relay_at(stage, j):
        return relay.at[stage, pl.ds(j * PIECE_ROWS, PIECE_ROWS)]

    def lens_to_prev(src, send, to):
        return remote(src, prev_len, send, len_recv.at[0], to)

    rows_in.wait()
    len_in.wait()
    own_swap = remote(rows_ref.at[core], rows_ref.at[core], own_send, own_recv, sibling)

    @pl.when(x == X - 1)
    def _():
        for (column, j), piece in PIECES.items():
            src, send, way = last_rows(piece), out_sem.at[piece], j % 2
            if column != X - 1:

                @pl.when((z < Z - 1) | (y < X - 1))
                def _():
                    to = device(column, y, z, core)
                    remote(src, relay_at(0, j), send, relay_sem.at[0, j], to).start()

            else:

                @pl.when(direct[way])
                def _():
                    to_prev(piece, src, send, device(0, y, target_of(z), core)).start()

                @pl.when(loops[way])
                def _():
                    to = device(column, y, onward[way], core)
                    remote(src, relay_at(1, j), send, relay_sem.at[1, j], to).start()

                @pl.when(crosses_y)
                def _():
                    to_prev(piece, src, send, device(0, y + 1, 0, core)).start()

        @pl.when(direct[0])
        def _():
            lens_to_prev(len_ref, len_send.at[0], device(0, y, target_of(z), core)).start()

        @pl.when(loops[0])
        def _():
            to = device(X - 1, y, onward[0], core)
            remote(len_ref, len_relay, len_send.at[0], len_recv.at[1], to).start()

        @pl.when(crosses_y)
        def _():
            lens_to_prev(len_ref, len_send.at[0], device(0, y + 1, 0, core)).start()

    own_swap.start()

    row_in_keys = lax.broadcasted_iota(jnp.int32, (1, 4 * GROUP_LEN), 1)
    key_position = (row_in_keys // (2 * GROUP_LEN)) * GROUP_LEN + row_in_keys % GROUP_LEN
    key_neighbour = (row_in_keys // GROUP_LEN) % 2

    def key_live(lens):
        length = jnp.where(
            key_neighbour == 0,
            jnp.broadcast_to(lens[:, 0:1], row_in_keys.shape),
            jnp.broadcast_to(lens[:, 1:2], row_in_keys.shape),
        )
        return key_position < length

    def project(rows, slot, at_row=0):
        into = pl.ds(at_row, rows.shape[0])

        for tile in range(kw_ref.shape[1] // 256):
            at = pl.ds(tile * 256, 256)
            keys_ref[slot, into, at] = jnp.dot(
                rows, kw_ref[:, at], preferred_element_type=jnp.float32
            ).astype(jnp.bfloat16)
            vals_ref[slot, into, at] = jnp.dot(
                rows, vw_ref[:, at], preferred_element_type=jnp.float32
            ).astype(jnp.bfloat16)

    def attend(first, count, slot, live):
        heads = [pl.ds(head * HEAD_DIM, HEAD_DIM) for head in range(q_ref.shape[1] // HEAD_DIM)]
        scores = [
            lax.dot_general(
                q_ref[first : first + count, at], keys_ref[slot, :, at],
                (((1,), (1,)), ((), ())), preferred_element_type=jnp.float32,
            )
            for at in heads
        ]
        scores = [jnp.where(live, each * HEAD_DIM ** (-0.5), MASK_FILL) for each in scores]
        most = [jnp.max(each, axis=-1, keepdims=True) for each in scores]
        weights = [jnp.exp(each - top) for each, top in zip(scores, most)]
        totals = [jnp.sum(each, axis=-1, keepdims=True) for each in weights]
        attention = [(each / total).astype(jnp.bfloat16) for each, total in zip(weights, totals)]
        return [
            jnp.dot(each, vals_ref[slot, :, at], preferred_element_type=jnp.float32).astype(jnp.bfloat16)
            for each, at in zip(attention, heads)
        ]

    def own_rows(group):
        return rows_ref[:, group].reshape(4 * GROUP_LEN, rows_ref.shape[-1])

    def step_own_project(group):
        if group == 0:
            kw_in.wait()
            vw_in.wait()
            arrived(rows_ref.at[other], own_recv)
        project(own_rows(group), group)

    def step_own_attend():
        q_in.wait()
        lens = len_ref[...]
        live0, live1 = key_live(lens[0:1]), key_live(lens[1:2])
        row = lax.broadcasted_iota(jnp.int32, (16, HEAD_DIM), 0)
        middle = attend(GROUP_LEN - 16, GROUP_LEN + 16, 0, live0)
        end = attend(2 * GROUP_LEN - 16, 16, 1, live1)
        for head, (mid, last) in enumerate(zip(middle, end)):
            at = pl.ds(head * HEAD_DIM, HEAD_DIM)
            own_edge[:, at] = mid[:16]
            out_ref[0, GROUP_LEN : 2 * GROUP_LEN - 16, at] = mid[16:GROUP_LEN]
            out_ref[0, 2 * GROUP_LEN - 16 :, at] = jnp.where(row < 15, mid[GROUP_LEN:], last)

    def own_work(step):
        if step == 0:
            step_own_project(0)
        elif step == 1:
            step_own_project(1)
        elif step == 2:
            step_own_attend()

    def forward(column):
        for j in range(COLUMN_PIECES[column]):
            piece, way = PIECES[column, j], j % 2
            src, send, got = relay_at(0, j), forward_sem.at[0, j], relay_sem.at[0, j]

            @pl.when(direct[way])
            def _():
                arrived(src, got)
                to_prev(piece, src, send, device(0, y, target_of(z), core)).start()

            @pl.when(loops[way])
            def _():
                arrived(src, got)
                to = device(column, y, onward[way], core)
                remote(src, relay_at(1, j), send, relay_sem.at[1, j], to).start()

            @pl.when(crosses_y)
            def _():
                arrived(src, got)
                to_prev(piece, src, send, device(0, y + 1, 0, core)).start()

    def pass_on(column, way):
        to = device(0, y, target_of(passed[way]), core)
        for j in range(way, COLUMN_PIECES[column], 2):
            arrived(relay_at(1, j), relay_sem.at[1, j])
            to_prev(PIECES[column, j], relay_at(1, j), forward_sem.at[1, j], to).start()
        if column == X - 1 and way == 0:
            arrived(len_relay, len_recv.at[1])
            lens_to_prev(len_relay, len_send.at[1], to).start()

    def send_across():
        to = device(x + 1, y, z, core)
        for piece in range(N_PIECES):
            to_prev(piece, last_rows(piece), out_sem.at[piece], to).start()
        lens_to_prev(len_ref, len_send.at[0], to).start()

    @pl.when((x < X - 1) & (z < HALF))
    def _():
        send_across()

    for column in columns:
        if column != X - 1:

            @pl.when(x == column)
            def _():
                forward(column)

    @pl.when((x < X - 1) & (z >= HALF))
    def _():
        send_across()

    for way in (0, 1):
        for column in columns:

            @pl.when((x == column) & passes[way])
            def _():
                pass_on(column, way)

    for step in range(3):
        own_work(step)

    left(rows_ref.at[core], own_send)

    @pl.when((x < X - 1) | (z < Z - 1) | (y < X - 1))
    def _():
        for piece in range(N_PIECES):
            left(last_rows(piece), out_sem.at[piece])
        left(len_ref, len_send.at[0])

    for column in columns:
        if column != X - 1:

            @pl.when((x == column) & ((z < Z - 1) | (y < X - 1)))
            def _():
                for j in range(COLUMN_PIECES[column]):
                    left(relay_at(0, j), forward_sem.at[0, j])

        for way in (0, 1):

            @pl.when((x == column) & passes[way])
            def _():
                for j in range(way, COLUMN_PIECES[column], 2):
                    left(relay_at(1, j), forward_sem.at[1, j])
                if column == X - 1 and way == 0:
                    left(len_relay, len_send.at[1])

    @pl.when(has_prev)
    def _():
        for index, column in enumerate(columns):
            for j in range(COLUMN_PIECES[column]):
                piece = PIECES[column, j]
                arrived(prev_rows(core, piece), prev_sem.at[piece])
            span = span_rows(core, column)
            remote(span, span, swap_send.at[index], swap_recv.at[index], sibling).start()
        arrived(prev_len, len_recv.at[0])
        half = prev_ref.shape[1]
        project(prev_ref[core], 2, pl.multiple_of(core * half, half))
        for index, column in enumerate(columns):
            arrived(span_rows(other, column), swap_recv.at[index])
        project(prev_ref[other], 2, pl.multiple_of(other * half, half))
        live = key_live(prev_len[1:2])
        row = lax.broadcasted_iota(jnp.int32, (16, HEAD_DIM), 0)
        edge = pl.ds(GROUP_LEN - 16, 16)
        for head, first in enumerate(attend(0, GROUP_LEN, 2, live)):
            at = pl.ds(head * HEAD_DIM, HEAD_DIM)
            out_ref[0, : GROUP_LEN - 16, at] = first[: GROUP_LEN - 16]
            out_ref[0, edge, at] = jnp.where(row < 15, first[GROUP_LEN - 16 :], own_edge[:, at])

    @pl.when(jnp.logical_not(has_prev))
    def _():
        row = lax.broadcasted_iota(jnp.int32, own_edge.shape, 0)
        out_ref[0, : GROUP_LEN - 16] = jnp.zeros((GROUP_LEN - 16, own_edge.shape[1]), jnp.bfloat16)
        edge = pl.ds(GROUP_LEN - 16, 16)
        out_ref[0, edge] = jnp.where(row < 15, jnp.zeros_like(row, jnp.bfloat16), own_edge[...])

    @pl.when(has_prev)
    def _():
        for index, column in enumerate(columns):
            left(span_rows(core, column), swap_send.at[index])


def write_out(from_ref, to_ref, sem):
    copy = pltpu.make_async_copy(from_ref, to_ref, sem)
    copy.start()
    copy.wait()


def shards(queries, encodings, neighbour_lengths, key_weight, value_weight):
    _, group_count, neighbours, half_rows, enc_width = encodings.shape
    tok_count, col_count = queries.shape[1:]
    bf16 = jnp.bfloat16
    anywhere = pl.BlockSpec(memory_space=pl.ANY)
    dma = pltpu.SemaphoreType.DMA
    attended = pl.pallas_call(
        kernel,
        out_shape=pltpu.VMEM(queries.shape, bf16),
        in_specs=[anywhere] * 5,
        out_specs=pl.BlockSpec(memory_space=pltpu.VMEM),
        scratch_shapes=[
            pltpu.VMEM((tok_count, col_count), bf16),
            pltpu.VMEM(key_weight.shape, bf16),
            pltpu.VMEM(value_weight.shape, bf16),
            pltpu.VMEM((group_count, neighbours), jnp.int32),
            pltpu.VMEM((group_count, neighbours), jnp.int32),
            pltpu.VMEM((2, group_count, neighbours, half_rows, enc_width), bf16),
            pltpu.VMEM((2, neighbours * half_rows, enc_width), bf16),
            pltpu.VMEM((3, 2 * neighbours * half_rows, col_count), bf16),
            pltpu.VMEM((3, 2 * neighbours * half_rows, col_count), bf16),
            pltpu.VMEM((16, col_count), bf16),
            pltpu.VMEM((2, MOST * PIECE_ROWS, enc_width), bf16),
            pltpu.VMEM((group_count, neighbours), jnp.int32),
            dma((5,)),
            dma((N_PIECES,)),
            dma((2, MOST)),
            dma((2, MOST)),
            dma((N_PIECES,)),
            dma((len(COLUMN_PIECES),)),
            dma((len(COLUMN_PIECES),)),
            dma((2,)),
            dma((2,)),
            dma,
            dma,
        ],
        compiler_params=pltpu.CompilerParams(
            collective_id=0, has_side_effects=True, vmem_limit_bytes=56 * 2**20
        ),
        name="attend_neighbours",
    )(queries, encodings, neighbour_lengths, key_weight, value_weight)
    return pl.pallas_call(
        write_out,
        out_shape=jax.ShapeDtypeStruct(queries.shape, bf16),
        in_specs=[anywhere],
        out_specs=anywhere,
        scratch_shapes=[dma],
        compiler_params=pltpu.CompilerParams(vmem_limit_bytes=2**20),
        name="write_out",
    )(attended)


def solution(mesh):
    placed = (
        P(None, ("seq", "fsdp"), "grp"),
        P(None, ("seq", "fsdp"), None, "grp", None),
        P(None, ("seq", "fsdp"), None),
        P(None, "grp"),
        P(None, "grp"),
    )
    return jax.shard_map(
        shards,
        mesh=mesh,
        in_specs=placed,
        out_specs=P(None, ("seq", "fsdp"), "grp"),
        check_vma=False,
    )
```
